256 devices in a mesh: dp: 8 (over z), frame: 8 (over x, core), audio: 4 (over y).
Axes of the slice: x: 4, y: 4, z: 8, core: 2. Of those that a mesh axis runs over, the one named last changes fastest.
Arguments:
- video_query: bfloat16 [8, 4096, 3072], P('dp', ('frame', 'audio')), may hold values from -72 to 72
- out_grad: bfloat16 [8, 4096, 3072], P('dp', ('frame', 'audio')), may hold values from -6 to 6
- audio_latents: bfloat16 [8, 1024, 3072], P('dp', 'audio'), may hold values from -6 to 6
- kv_weight: bfloat16 [3072, 2, 3072], P(None, None, 'frame'), may hold values from -0.4375 to 0.4375
- video_length: int32 [8], P('dp'), may hold values from 1024 to 4096, as said below
- audio_length: int32 [8], P('dp'), may hold values from 128 to 1024, as said below
- align_list: int32 [8, 32, 2], P('dp'), may hold values from 0 to 15, as said below
Outputs:
- attended: bfloat16 [8, 4096, 3072], P('dp', ('frame', 'audio'))
- query_grad: bfloat16 [8, 4096, 3072], P('dp', ('frame', 'audio'))
- kv_weight_grad: float32 [3072, 2, 3072], P(('dp', 'audio'), None, 'frame')
The draws below stay inside these ranges and needn't reach their ends.
Inputs may be any that keep to these rules, and one draw needn't show every extreme that they name: `video_length`: one clip of every draw has all 4096 tokens live. `audio_length`: one clip of every draw has all 1024 latents live. `align_list`: for clip c and query block b the 2 entries are distinct and each is below ceil(audio_length[c] / 64); the first is b * ceil(audio_length[c] / 64) // 32.
All inputs are finite; a program needn't handle non-finite values.
Results may differ from the reference program's by a relative error of at most 0.004.
The reference program's roundings to bfloat16 on the way count: a program that leaves them out, or rounds other values in their place, can miss the bound.
Values may be sent and summed in bfloat16 or wider, within the bound.
No kernel may reach another device: no remote copies, remote signals or barrier semaphores. Data moves between devices by JAX's collectives and lax.ppermute only.
A program may use at most 128 MiB of HBM per device.

```python
import jax
import jax.numpy as jnp
from jax import lax

D = 3072
HEADS = 24
HD = 128
QB = 128
KB = 64
NLIST = 2
CLIPS = 8
TV = 4096
TA = 1024
NQB = 32
NKB = 16


def skewed_length(key, lowest, highest):
    first, second, third = jax.random.split(key, 3)
    draw_one = jax.random.randint(first, (CLIPS,), lowest, highest + 1)
    draw_two = jax.random.randint(second, (CLIPS,), lowest, highest + 1)
    picked = jax.random.randint(third, (), 0, CLIPS)
    lengths = jnp.minimum(draw_one, draw_two)
    return jnp.where(jnp.arange(CLIPS) == picked, highest, lengths).astype(jnp.int32)


def lengths_and_lists(key):
    video_key = jax.random.fold_in(key, 101)
    audio_key = jax.random.fold_in(key, 202)
    list_key = jax.random.fold_in(key, 303)
    video_live = skewed_length(video_key, TV // 4, TV)
    audio_live = skewed_length(audio_key, NLIST * KB, TA)
    audio_blocks = (audio_live + KB - 1) // KB
    centers = jnp.arange(NQB, dtype=jnp.int32)[None, :] * audio_blocks[:, None] // NQB
    noise = jax.random.randint(list_key, (CLIPS, NQB, NKB), 0, 2 ** 20)
    block_ids = jnp.arange(NKB, dtype=jnp.int32)[None, None, :]
    ranked = jnp.where(block_ids < audio_blocks[:, None, None], noise * NKB + block_ids, 2 ** 28 + block_ids)
    ranked = jnp.where(block_ids == centers[:, :, None], -1, ranked)
    order = jnp.argsort(ranked, axis=-1, stable=True)[:, :, :NLIST]
    return (video_live, audio_live, order.astype(jnp.int32))


def draw_video_length(key, part):
    return lengths_and_lists(key)[0]


def draw_audio_length(key, part):
    return lengths_and_lists(key)[1]


def draw_align_list(key, part):
    return lengths_and_lists(key)[2]


def draw_video_query(key, part):
    first = jax.random.fold_in(jax.random.fold_in(key, 11), 0)
    values = jnp.clip(jax.random.normal(first, (CLIPS, TV, D), jnp.float32), -6.0, 6.0) * 0.25
    return values.astype(jnp.bfloat16)


def block_levels(own_key, dims, cuts, least, top_value):
    level, own = 1.0, jax.random.fold_in(own_key, 6)
    for axis_at, blocks in cuts:
        draws = jnp.exp(jax.random.uniform(jax.random.fold_in(own, axis_at), (blocks,), jnp.float32, least / len(cuts), top_value / len(cuts)))
        level = level * jnp.repeat(draws, dims[axis_at] // blocks).reshape([-1 if axis == axis_at else 1 for axis in range(len(dims))])
    return level


def scatter_about(key, shape, deviation, reach, pieces=(), kind=jnp.bfloat16):
    result = jax.random.normal(key, shape, jnp.float32) * deviation
    if len(pieces) > 0:
        result = block_levels(key, shape, pieces, -0.22, 0.18) * result
    return jnp.clip(result, min=-reach, max=reach).astype(kind)


def setup_inputs(seed: int = 0) -> dict:
    keys = jax.random.split(jax.random.key(seed), 8)
    return {
        "video_query": draw_video_query(jax.random.fold_in(keys[7], 71), 0),
        "out_grad": scatter_about(keys[1], (CLIPS, TV, D), 1.0, 6.0, ((0, 8), (1, 32))),
        "audio_latents": scatter_about(keys[2], (CLIPS, TA, D), 1.0, 6.0, ((0, 8), (1, 4))),
        "kv_weight": scatter_about(keys[3], (D, 2, D), (D // 16) ** -0.5, 0.4375, ((2, 8),)),
        "video_length": draw_video_length(jax.random.fold_in(keys[7], 71), 0),
        "audio_length": draw_audio_length(jax.random.fold_in(keys[7], 71), 0),
        "align_list": draw_align_list(jax.random.fold_in(keys[7], 71), 0),
    }


def clip_pass(kv_weight, inputs):
    query_all, grad_all, latents, video_live, audio_live, block_lists = inputs
    scaling = HD ** -0.5
    projected = jnp.dot(latents, kv_weight.reshape(D, 2 * D), preferred_element_type=jnp.float32).astype(jnp.bfloat16)
    projected = lax.optimization_barrier(projected)
    blocks = projected.reshape(NKB, KB, 2, HEADS, HD)
    query_blocks = query_all.reshape(NQB, QB, HEADS, HD)
    grad_blocks = grad_all.reshape(NQB, QB, HEADS, HD)

    def advance(totals, index):
        listed = block_lists[index]
        chosen = jnp.take(blocks, listed, axis=0).reshape(NLIST * KB, 2, HEADS, HD).astype(jnp.float32)
        key_rows = chosen[:, 0]
        value_rows = chosen[:, 1]
        key_index = (listed[:, None] * KB + jnp.arange(KB, dtype=jnp.int32)[None, :]).reshape(NLIST * KB)
        key_live = key_index < audio_live
        row_index = index * QB + jnp.arange(QB, dtype=jnp.int32)
        live_rows = row_index < video_live
        query_rows = query_blocks[index].astype(jnp.float32)
        grad_rows = grad_blocks[index].astype(jnp.float32)
        scores = jnp.einsum("qhd,khd->hqk", query_rows, key_rows) * scaling
        scores = jnp.where(key_live[None, None, :], scores, -1e30)
        scores = scores - jnp.max(scores, axis=-1, keepdims=True)
        weights = jnp.exp(scores)
        probability = weights / jnp.sum(weights, axis=-1, keepdims=True)
        probability = jnp.where(live_rows[None, :, None], probability, 0.0)
        prob_low = lax.optimization_barrier(probability.astype(jnp.bfloat16)).astype(jnp.float32)
        output = jnp.einsum("hqk,khd->qhd", prob_low, value_rows).astype(jnp.bfloat16)
        prob_grad = jnp.einsum("qhd,khd->hqk", grad_rows, value_rows)
        row_dot = jnp.sum(probability * prob_grad, axis=-1, keepdims=True)
        score_grad = probability * (prob_grad - row_dot)
        score_grad = lax.optimization_barrier(score_grad.astype(jnp.bfloat16)).astype(jnp.float32)
        query_part = (jnp.einsum("hqk,khd->qhd", score_grad, key_rows) * scaling).astype(jnp.bfloat16)
        key_part = jnp.einsum("hqk,qhd->khd", score_grad, query_rows) * scaling
        value_part = jnp.einsum("hqk,qhd->khd", prob_low, grad_rows)
        both = jnp.stack([key_part, value_part], axis=1).reshape(NLIST, KB, 2, HEADS, HD)
        totals = totals.at[listed].add(both)
        return totals, (output.reshape(QB, D), query_part.reshape(QB, D))

    totals = jnp.zeros((NKB, KB, 2, HEADS, HD), jnp.float32)
    totals, (output, query_part) = lax.scan(advance, totals, jnp.arange(NQB, dtype=jnp.int32))
    kv_grad = totals.reshape(TA, 2 * D).astype(jnp.bfloat16)
    weight_part = lax.dot_general(latents, kv_grad, (((0,), (0,)), ((), ())), preferred_element_type=jnp.float32)
    return output.reshape(TV, D), query_part.reshape(TV, D), weight_part


def reference(video_query, out_grad, audio_latents, kv_weight, video_length, audio_length, align_list):
    def per_clip(running, inputs):
        attended, query_grad, weight_part = clip_pass(kv_weight, inputs)
        return running + weight_part, (attended, query_grad)

    running = jnp.zeros((D, 2 * D), jnp.float32)
    running, (attended, query_grad) = lax.scan(per_clip, running, (video_query, out_grad, audio_latents, video_length, audio_length, align_list))
    return attended, query_grad, (running * (1.0 / CLIPS)).reshape(D, 2, D)
```

```python
import jax
import jax.numpy as jnp
from jax import lax
from jax.experimental import pallas as pl
from jax.experimental.pallas import tpu as pltpu
from jax.sharding import PartitionSpec as P


D = 3072
HD = 128
QB = 128
KB = 64
NLIST = 2
SCALING = HD ** (-0.5)
LOG2_E = 1.4426950408889634
BF16 = jnp.bfloat16
F32 = jnp.float32


VMEM = pl.BlockSpec(memory_space=pltpu.VMEM)
SMEM = pl.BlockSpec(memory_space=pltpu.SMEM)
ANY = pl.BlockSpec(memory_space=pl.ANY)


def shifted(array, axis, by):
    count = lax.axis_size(axis)
    return lax.ppermute(array, axis, [(i, (i + by) % count) for i in range(count)])


def pack_kernel(query, grad, out):
    width = out.shape[3]
    for j in range(out.shape[0]):
        out[j, 0] = query[:, j * width : (j + 1) * width]
        out[j, 1] = grad[:, j * width : (j + 1) * width]


def pack(query, grad, frames):
    rows, width = query.shape
    return pl.pallas_call(
        pack_kernel,
        out_shape=jax.ShapeDtypeStruct((frames, 2, rows, width // frames), query.dtype),
        in_specs=[VMEM, VMEM],
        out_specs=VMEM,
        name="pack",
    )(query, grad)


def unpack_kernel(pieces, attended, query_grad):
    width = pieces.shape[3]
    for j in range(pieces.shape[0]):
        attended[:, j * width : (j + 1) * width] = pieces[j, 0]
        query_grad[:, j * width : (j + 1) * width] = pieces[j, 1]


def unpack(pieces):
    frames, _, rows, width = pieces.shape
    whole = jax.ShapeDtypeStruct((rows, width * frames), pieces.dtype)
    return pl.pallas_call(
        unpack_kernel,
        out_shape=[whole, whole],
        in_specs=[VMEM],
        out_specs=[VMEM, VMEM],
        name="unpack",
    )(pieces)


def turn_kernel(ids, latents, own, *refs):
    sends, turned = refs[:-1], refs[-1]
    _, count, rows, _ = own.shape
    audio_count = len(sends) + 1
    width = rows * audio_count
    parity = lax.rem(ids[1], 2)
    for group in range(2):
        for j in range(count):
            owner = 2 * j + (parity if group == 0 else 1 - parity)
            turned[...] = latents[:, pl.ds(pl.multiple_of(owner * width, HD), width)].T
            own[group, j] = turned[pl.ds(pl.multiple_of(ids[0] * rows, 16), rows), :]

            @pl.when(ids[2] == group)
            def _():
                for k in range(1, audio_count):
                    first = pl.multiple_of(lax.rem(ids[0] + k, audio_count) * rows, 16)
                    sends[k - 1][j] = turned[pl.ds(first, rows), :]


def turn(ids, latents, clips, audio_count):
    count, width = latents.shape
    rows = width // (clips * audio_count)
    shape = (clips // 2, rows, count)
    return pl.pallas_call(
        turn_kernel,
        out_shape=[jax.ShapeDtypeStruct((2, *shape), latents.dtype)]
        + [jax.ShapeDtypeStruct(shape, latents.dtype)] * (audio_count - 1),
        in_specs=[SMEM, VMEM],
        out_specs=[VMEM] * audio_count,
        scratch_shapes=[pltpu.VMEM((rows * audio_count, count), latents.dtype)],
        name="turn",
    )(ids, latents)


def dot(left, right, left_dim, right_dim):
    return lax.dot_general(
        left, right, (((left_dim,), (right_dim,)), ((), ())), preferred_element_type=F32
    )


def attend_kernel(audio_count, heads, ids, video_live, audio_live, lists, *refs):
    refs = list(refs)
    take = lambda n: [refs.pop(0) for _ in range(n)]
    (arrived,), tables = take(1), take(audio_count)
    (results,), grads = take(1), take(2 * audio_count)
    rows_in, table, rows_out = take(3)
    sums = take(2 * heads)
    in_sem, table_sem, out_sem = take(3)
    frames = arrived.shape[0]
    share = tables[0].shape[0]
    here = ids[0]

    copies = []
    for k in range(audio_count):
        at = pl.multiple_of(lax.rem(here + audio_count - k, audio_count) * share, share)
        copies.append(
            pltpu.make_async_copy(tables[k], table.at[pl.ds(at, share), :], table_sem.at[k])
        )
    copies.append(pltpu.make_async_copy(arrived, rows_in, in_sem))
    for copy in copies:
        copy.start()
    for part in sums:
        part[...] = jnp.zeros_like(part)
    for copy in copies:
        copy.wait()

    key_row = lax.broadcasted_iota(jnp.int32, (NLIST * KB, 1), 0)
    query_lane = lax.broadcasted_iota(jnp.int32, (1, QB), 1)

    def one(k):
        index = k * audio_count + here
        first = pl.multiple_of(lists[NLIST * index] * KB, KB)
        second = pl.multiple_of(lists[NLIST * index + 1] * KB, KB)
        key_index = jnp.where(key_row < KB, first + key_row, second + key_row - KB)
        allowed = key_index < audio_live[0]
        live = query_lane + index * QB < video_live[0]
        parts = []
        for h in range(heads):
            cols = slice(h * HD, (h + 1) * HD)
            vcols = slice((heads + h) * HD, (heads + h + 1) * HD)
            query = rows_in[k, 0, :, cols]
            grad = rows_in[k, 1, :, cols]
            key = jnp.concatenate(
                [table[pl.ds(first, KB), cols], table[pl.ds(second, KB), cols]], axis=0
            )
            value = jnp.concatenate(
                [table[pl.ds(first, KB), vcols], table[pl.ds(second, KB), vcols]], axis=0
            )
            scores = dot(key, query, 1, 1)
            prob_grad = dot(value, grad, 1, 1)
            scores = jnp.where(allowed, scores, -1e30)
            scores = scores - jnp.max(scores, axis=0, keepdims=True)
            weights = jnp.exp2(scores * (SCALING * LOG2_E))
            inverse = 1.0 / jnp.sum(weights, axis=0, keepdims=True)
            probability = weights * jnp.where(live, inverse, 0.0)
            prob_low = probability.astype(BF16)
            row_dot = jnp.sum(probability * prob_grad, axis=0, keepdims=True)
            score_grad = (probability * (prob_grad - row_dot)).astype(BF16)
            output = dot(prob_low, value, 0, 0).astype(BF16)
            query_part = (dot(score_grad, key, 0, 0) * SCALING).astype(BF16)
            key_part = dot(score_grad, query, 1, 0) * SCALING
            value_part = dot(prob_low, grad, 1, 0)
            parts.append((output, query_part, key_part, value_part))
        return first, second, parts

    def finish(k, first, second, parts):
        for h, (output, query_part, key_part, value_part) in enumerate(parts):
            cols = slice(h * HD, (h + 1) * HD)
            rows_out[k, 0, :, cols] = output
            rows_out[k, 1, :, cols] = query_part
            for into, part in ((sums[h], key_part), (sums[heads + h], value_part)):
                into[pl.ds(first, KB), :] += part[:KB]
                into[pl.ds(second, KB), :] += part[KB:]

    def block(step, carry):
        made = [(2 * step + i, *one(2 * step + i)) for i in range(2)]
        for entry in made:
            finish(*entry)
        return carry

    lax.fori_loop(0, frames // 2, block, 0)

    copy = pltpu.make_async_copy(rows_out, results, out_sem)
    copy.start()
    for k in range(audio_count):
        at = pl.multiple_of(lax.rem(here + k, audio_count) * share, share)
        for half in range(2):
            into = grads[2 * k + half]
            for h in range(heads):
                part = sums[half * heads + h][pl.ds(at, share), :]
                into[:, h * HD : (h + 1) * HD] = part.astype(into.dtype)
    copy.wait()


def attend(ids, video_live, audio_live, lists, arrived, tables):
    audio_count = len(tables)
    share, width = tables[0].shape
    heads = width // (2 * HD)
    total = share * audio_count

    def kernel(*refs):
        attend_kernel(audio_count, heads, *refs)

    results, *grads = pl.pallas_call(
        kernel,
        out_shape=[jax.ShapeDtypeStruct(arrived.shape, BF16)]
        + [jax.ShapeDtypeStruct((share, width // 2), F32)] * 2
        + [jax.ShapeDtypeStruct((share, width // 2), BF16)] * (2 * audio_count - 2),
        in_specs=[SMEM] * 4 + [ANY] * (1 + audio_count),
        out_specs=[ANY] + [VMEM] * (2 * audio_count),
        scratch_shapes=[
            pltpu.VMEM(arrived.shape, BF16),
            pltpu.VMEM((total, width), BF16),
            pltpu.VMEM(arrived.shape, BF16),
        ]
        + [pltpu.VMEM((total, HD), F32)] * (2 * heads)
        + [
            pltpu.SemaphoreType.DMA,
            pltpu.SemaphoreType.DMA((audio_count,)),
            pltpu.SemaphoreType.DMA,
        ],
        name="attend",
    )(ids, video_live, audio_live, lists, arrived, *tables)
    return results, grads


def product_kernel(scale, hops, ids, own, *refs):
    refs = list(refs)
    take = lambda n: [refs.pop(0) for _ in range(n)]
    mine, other, grads = take(hops), take(hops), take(hops + 1)
    kept, sent, turned, sems = take(4)
    core = ids[2]
    copies = []
    for k in range(hops):
        for i, (ref, at) in enumerate(((mine[k], core), (other[k], 1 - core))):
            copies.append(pltpu.make_async_copy(ref, turned.at[k, at], sems.at[k, i]))
    for copy in copies:
        copy.start()
    for copy in copies:
        copy.wait()
    for group, out in enumerate((kept, sent)):
        for j in range(out.shape[0]):
            total = dot(own[group, j], grads[0][...], 1, 0)
            for k in range(hops):
                total += dot(turned[k, group, j], grads[k + 1][...], 1, 0)
            out[j] = (total * scale).astype(out.dtype)


def product(ids, own, mine, other, grads, scale):
    _, count, rows, _ = own.shape
    width = grads[0].shape[1]
    hops = len(mine)

    def kernel(*refs):
        product_kernel(scale, hops, *refs)

    return pl.pallas_call(
        kernel,
        out_shape=[
            jax.ShapeDtypeStruct((count, rows, width), F32),
            jax.ShapeDtypeStruct((count, rows, width), BF16),
        ],
        in_specs=[SMEM, VMEM] + [ANY] * (2 * hops) + [VMEM] * (hops + 1),
        out_specs=[VMEM, VMEM],
        scratch_shapes=[
            pltpu.VMEM((hops, *own.shape), own.dtype),
            pltpu.SemaphoreType.DMA((hops, 2)),
        ],
        name="product",
    )(ids, own, *mine, *other, *grads)


def merge_kernel(ids, key_kept, value_kept, key_came, value_came, *outs):
    count = len(outs)
    width = key_kept.shape[2]
    for s in range(count):
        at = lax.rem(lax.div(ids[1], 2) + s, count)
        key = key_kept[at] + key_came[at].astype(F32)
        value = value_kept[at] + value_came[at].astype(F32)
        outs[s][:, :width] = key.astype(outs[s].dtype)
        outs[s][:, width:] = value.astype(outs[s].dtype)


def merge(ids, key_kept, value_kept, key_came, value_came):
    count, rows, width = key_kept.shape
    shape = (rows, 2 * width)
    return pl.pallas_call(
        merge_kernel,
        out_shape=[jax.ShapeDtypeStruct(shape, F32)]
        + [jax.ShapeDtypeStruct(shape, BF16)] * (count - 1),
        in_specs=[SMEM] + [VMEM] * 4,
        out_specs=[VMEM] * count,
        name="merge",
    )(ids, key_kept, value_kept, key_came, value_came)


def total_of(pieces):
    total = pieces[0]
    for piece in pieces[1:]:
        total = total + piece.astype(F32)
    return total


def to_owners(array, axis):
    return lax.all_to_all(array, axis, split_axis=0, concat_axis=0, tiled=True)


def per_device(
    video_query, out_grad, audio_latents, kv_weight, video_length, audio_length, align_list
):
    frames = lax.axis_size("frame")
    audio_count = lax.axis_size("audio")
    clips = lax.axis_size("dp")
    local_width = kv_weight.shape[2]
    latents = audio_latents[0]
    ids = [
        lax.axis_index("audio"),
        lax.axis_index("dp"),
        lax.rem(lax.axis_index("frame"), 2),
    ]
    ids = jnp.stack(ids).astype(jnp.int32)
    beside = [(i, i ^ 1) for i in range(frames)]
    before = [(i, i ^ 1) for i in range(clips)]
    after = [(i, (((i + 1) % clips) ^ 1) - 1) for i in range(clips)]
    after = [(i, j % clips) for i, j in after]
    hops = range(1, audio_count)

    packed = pack(video_query[0], out_grad[0], frames)
    arrived = to_owners(packed, "frame")
    projected = jnp.dot(
        latents, kv_weight.reshape(D, 2 * local_width), preferred_element_type=F32
    ).astype(BF16)
    tables = [projected]
    for k in hops:
        tables.append(shifted(projected, "audio", k))
    held, *pieces = turn(ids, latents, clips, audio_count)
    turned = []
    for k in hops:
        turned.append(shifted(pieces[k - 1], "audio", k))

    results, grads = attend(
        ids, video_length, audio_length, align_list.reshape(-1), arrived, tables
    )
    own = []
    for half in (1, 0):
        added = [grads[half]]
        for k in hops:
            added.append(shifted(grads[2 * k + half], "audio", k))
        own.append(total_of(added).astype(BF16))
    results = to_owners(results, "frame")
    swapped = []
    for k in hops:
        swapped.append(lax.ppermute(turned[k - 1], "frame", beside))
    halves = []
    for mine, partner in zip(own, (before, after)):
        shares = [mine]
        for k in hops:
            shares.append(shifted(mine, "audio", k))
        kept, sent = product(ids, held, turned, swapped, shares, 1.0 / clips)
        halves.append((kept, lax.ppermute(sent, "dp", partner)))
    (value_kept, value_came), (key_kept, key_came) = halves
    merged = merge(ids, key_kept, value_kept, key_came, value_came)
    parts = [merged[0]]
    for k in range(1, len(merged)):
        parts.append(shifted(merged[k], "dp", 2 * k))
    weight_grad = total_of(parts).reshape(-1, 2, local_width)
    attended, query_grad = unpack(results)
    return attended[None], query_grad[None], weight_grad


def solution(mesh):
    return jax.shard_map(
        per_device,
        mesh=mesh,
        in_specs=(
            P("dp", ("frame", "audio"), None),
            P("dp", ("frame", "audio"), None),
            P("dp", "audio", None),
            P(None, None, "frame"),
            P("dp"),
            P("dp"),
            P("dp", None, None),
        ),
        out_specs=(
            P("dp", ("frame", "audio"), None),
            P("dp", ("frame", "audio"), None),
            P(("dp", "audio"), None, "frame"),
        ),
        check_vma=False,
    )
```

```python
import jax
import jax.numpy as jnp
from jax import lax
from jax.experimental import pallas as pl
from jax.experimental.pallas import tpu as pltpu
from jax.sharding import PartitionSpec as P


D = 3072
HD = 128
QB = 128
KB = 64
NLIST = 2
SCALING = HD ** (-0.5)
LOG2_E = 1.4426950408889634
BF16 = jnp.bfloat16
F32 = jnp.float32


VMEM = pl.BlockSpec(memory_space=pltpu.VMEM)
SMEM = pl.BlockSpec(memory_space=pltpu.SMEM)
ANY = pl.BlockSpec(memory_space=pl.ANY)


def shifted(array, axis, by):
    count = lax.axis_size(axis)
    return lax.ppermute(array, axis, [(i, (i + by) % count) for i in range(count)])


def pack_kernel(query, grad, out):
    width = out.shape[3]
    for j in range(out.shape[0]):
        out[j, 0] = query[:, j * width : (j + 1) * width]
        out[j, 1] = grad[:, j * width : (j + 1) * width]


def pack(query, grad, frames):
    rows, width = query.shape
    return pl.pallas_call(
        pack_kernel,
        out_shape=jax.ShapeDtypeStruct((frames, 2, rows, width // frames), query.dtype),
        in_specs=[VMEM, VMEM],
        out_specs=VMEM,
        name="pack",
    )(query, grad)


def unpack_kernel(pieces, attended, query_grad):
    width = pieces.shape[3]
    for j in range(pieces.shape[0]):
        attended[:, j * width : (j + 1) * width] = pieces[j, 0]
        query_grad[:, j * width : (j + 1) * width] = pieces[j, 1]


def unpack(pieces):
    frames, _, rows, width = pieces.shape
    whole = jax.ShapeDtypeStruct((rows, width * frames), pieces.dtype)
    return pl.pallas_call(
        unpack_kernel,
        out_shape=[whole, whole],
        in_specs=[VMEM],
        out_specs=[VMEM, VMEM],
        name="unpack",
    )(pieces)


def turn_kernel(audio_count, ids, latents, own, near, far, turned):
    rows = turned.shape[0] // audio_count
    count = own.shape[0] // rows
    width = rows * audio_count
    core = ids[2]

    def part(ahead):
        at = lax.rem(ids[0] + ahead, audio_count) * rows
        return turned[pl.ds(pl.multiple_of(at, 16), rows), :]

    for j in range(count):
        turned[...] = latents[:, j * width : (j + 1) * width].T
        own[j * rows : (j + 1) * rows] = part(0)
        near[j * rows : (j + 1) * rows] = part(1 + core * (audio_count - 2))
        half, place = divmod(j, count // 2)

        @pl.when(core == half)
        def _():
            far[place * rows : (place + 1) * rows] = part(2)


def turn(ids, latents, clips, audio_count):
    count, width = latents.shape
    share = width // audio_count

    def kernel(*refs):
        turn_kernel(audio_count, *refs)

    return pl.pallas_call(
        kernel,
        out_shape=[
            jax.ShapeDtypeStruct((share, count), latents.dtype),
            jax.ShapeDtypeStruct((share, count), latents.dtype),
            jax.ShapeDtypeStruct((share // 2, count), latents.dtype),
        ],
        in_specs=[SMEM, VMEM],
        out_specs=[VMEM] * 3,
        scratch_shapes=[pltpu.VMEM((width // clips, count), latents.dtype)],
        name="turn",
    )(ids, latents)


def dot(left, right, left_dim, right_dim):
    return lax.dot_general(
        left, right, (((left_dim,), (right_dim,)), ((), ())), preferred_element_type=F32
    )


def attend_kernel(audio_count, heads, ids, rows_in, *refs):
    refs = list(refs)
    take = lambda n: [refs.pop(0) for _ in range(n)]
    tables, (rows_out,), grads = take(5), take(1), take(audio_count)
    (table,), sums, (table_sem,) = take(1), take(2 * heads), take(1)
    share = tables[0].shape[0]
    here = ids[0]
    step = pl.program_id(0)
    count = rows_in.shape[0]

    @pl.when(step == 0)
    def _():
        copies = []
        places = ((0, 0), (audio_count - 1, 0), (1, 0), (2, 0), (2, share // 2))
        for i, (ahead, extra) in enumerate(places):
            at = lax.rem(here + ahead, audio_count) * share + extra
            at = pl.ds(pl.multiple_of(at, share // 2), tables[i].shape[0])
            copies.append(pltpu.make_async_copy(tables[i], table.at[at, :], table_sem.at[i]))
        for copy in copies:
            copy.start()
        for part in sums:
            part[...] = jnp.zeros_like(part)
        for copy in copies:
            copy.wait()

    key_row = lax.broadcasted_iota(jnp.int32, (NLIST * KB, 1), 0)
    query_lane = lax.broadcasted_iota(jnp.int32, (1, QB), 1)

    def one(k):
        index = (step * count + k) * audio_count + here
        first = pl.multiple_of(ids[5 + NLIST * index] * KB, KB)
        second = pl.multiple_of(ids[6 + NLIST * index] * KB, KB)
        key_index = jnp.where(key_row < KB, first + key_row, second + key_row - KB)
        allowed = key_index < ids[4]
        live = query_lane + index * QB < ids[3]
        parts = []
        for h in range(heads):
            cols = slice(h * HD, (h + 1) * HD)
            vcols = slice((heads + h) * HD, (heads + h + 1) * HD)
            query = rows_in[k, 0, :, cols]
            grad = rows_in[k, 1, :, cols]
            key = jnp.concatenate(
                [table[pl.ds(first, KB), cols], table[pl.ds(second, KB), cols]], axis=0
            )
            value = jnp.concatenate(
                [table[pl.ds(first, KB), vcols], table[pl.ds(second, KB), vcols]], axis=0
            )
            scores = dot(key, query, 1, 1)
            prob_grad = dot(value, grad, 1, 1)
            scores = jnp.where(allowed, scores, -1e30)
            scores = scores - jnp.max(scores, axis=0, keepdims=True)
            weights = jnp.exp2(scores * (SCALING * LOG2_E))
            inverse = 1.0 / jnp.sum(weights, axis=0, keepdims=True)
            probability = weights * jnp.where(live, inverse, 0.0)
            prob_low = probability.astype(BF16)
            row_dot = jnp.sum(probability * prob_grad, axis=0, keepdims=True)
            score_grad = (probability * (prob_grad - row_dot)).astype(BF16)
            output = dot(prob_low, value, 0, 0).astype(BF16)
            query_part = (dot(score_grad, key, 0, 0) * SCALING).astype(BF16)
            key_part = dot(score_grad, query, 1, 0) * SCALING
            value_part = dot(prob_low, grad, 1, 0)
            parts.append((output, query_part, key_part, value_part))
        return first, second, parts

    def finish(k, first, second, parts):
        for h, (output, query_part, key_part, value_part) in enumerate(parts):
            cols = slice(h * HD, (h + 1) * HD)
            rows_out[k, 0, :, cols] = output
            rows_out[k, 1, :, cols] = query_part
            for into, part in ((sums[h], key_part), (sums[heads + h], value_part)):
                into[pl.ds(first, KB), :] += part[:KB]
                into[pl.ds(second, KB), :] += part[KB:]

    made = [(k, *one(k)) for k in range(count)]
    for entry in made:
        finish(*entry)

    @pl.when(step == pl.num_programs(0) - 1)
    def _():
        for k in range(audio_count):
            at = pl.multiple_of(lax.rem(here + k, audio_count) * share, share)
            for c, total in enumerate(sums):
                half, h = divmod(c, heads)
                place = half + (1 - 2 * half) * (1 - lax.rem(ids[1], 2))
                cols = pl.ds(pl.multiple_of((place * heads + h) * HD, HD), HD)
                grads[k][:, cols] = total[pl.ds(at, share), :].astype(grads[k].dtype)


def attend(ids, arrived, tables, audio_count):
    share, width = tables[0].shape
    heads = width // (2 * HD)
    total = share * audio_count
    count = 2
    rows = pl.BlockSpec((count, *arrived.shape[1:]), lambda i: (i, 0, 0, 0))
    part = pl.BlockSpec((share, width), lambda i: (0, 0))

    def kernel(*refs):
        attend_kernel(audio_count, heads, *refs)

    results, *grads = pl.pallas_call(
        kernel,
        grid=(arrived.shape[0] // count,),
        out_shape=[jax.ShapeDtypeStruct(arrived.shape, BF16)]
        + [jax.ShapeDtypeStruct((share, width), F32)]
        + [jax.ShapeDtypeStruct((share, width), BF16)] * (audio_count - 1),
        in_specs=[SMEM, rows] + [ANY] * len(tables),
        out_specs=[rows] + [part] * audio_count,
        scratch_shapes=[pltpu.VMEM((total, width), BF16)]
        + [pltpu.VMEM((total, HD), F32)] * (2 * heads)
        + [pltpu.SemaphoreType.DMA((len(tables),))],
        compiler_params=pltpu.CompilerParams(dimension_semantics=("arbitrary",)),
        name="attend",
    )(ids, arrived, *tables)
    return results, grads


def assemble_kernel(ids, near, far, near_swapped, far_swapped, out):
    half, depth = far.shape
    core = ids[2]
    middle = slice(depth, 2 * depth)
    out[pl.ds(pl.multiple_of(core * half, 16), half), middle] = far[...]
    out[pl.ds(pl.multiple_of((1 - core) * half, 16), half), middle] = far_swapped[...]

    @pl.when(core == 0)
    def _():
        out[:, :depth] = near[...]
        out[:, 2 * depth :] = near_swapped[...]

    @pl.when(core == 1)
    def _():
        out[:, :depth] = near_swapped[...]
        out[:, 2 * depth :] = near[...]


def assemble(ids, near, *parts):
    rows, depth = near.shape
    return pl.pallas_call(
        assemble_kernel,
        out_shape=jax.ShapeDtypeStruct((rows, depth * 3), near.dtype),
        in_specs=[SMEM] + [VMEM] * 4,
        out_specs=VMEM,
        name="assemble",
    )(ids, near, *parts)


def first_product_kernel(held, rest, paired_held, came, *refs):
    grads, (out, table) = refs[:-2], refs[-2:]
    depth = came.shape[0]
    for k, grad in enumerate(grads[1:]):
        table[k * depth : (k + 1) * depth, :] = grad[...]
    total = dot(held[...], grads[0][...], 1, 0) + dot(paired_held[...], came[...], 1, 0)
    out[...] = total + dot(rest[...], table[...], 1, 0)


def first_product(held, rest, paired_held, came, grads):
    shape = (held.shape[0], came.shape[1])
    return pl.pallas_call(
        first_product_kernel,
        out_shape=jax.ShapeDtypeStruct(shape, F32),
        in_specs=[VMEM] * (4 + len(grads)),
        out_specs=VMEM,
        scratch_shapes=[pltpu.VMEM((rest.shape[1], shape[1]), BF16)],
        name="first_product",
    )(held, rest, paired_held, came, *grads)


def second_product_kernel(scale, hops, ids, so_far, rest, *refs):
    grads, outs, (whole, table) = refs[:hops], refs[hops:-2], refs[-2:]
    depth = grads[0].shape[0]
    for k, grad in enumerate(grads):
        table[k * depth : (k + 1) * depth, :] = grad[...]
    whole[...] = (so_far[...] + dot(rest[...], table[...], 1, 0)) * scale
    count, rows = len(outs), outs[0].shape[0]
    for k in range(count):
        at = pl.multiple_of(lax.rem(ids[1] + k, count) * rows, 16)
        outs[k][...] = whole[pl.ds(at, rows), :].astype(outs[k].dtype)


def second_product(ids, so_far, rest, grads, count, scale):
    rows, width = so_far.shape

    def kernel(*refs):
        second_product_kernel(scale, len(grads), *refs)

    shape = (rows // count, width)
    return pl.pallas_call(
        kernel,
        out_shape=[jax.ShapeDtypeStruct(shape, F32)]
        + [jax.ShapeDtypeStruct(shape, BF16)] * (count - 1),
        in_specs=[SMEM] + [VMEM] * (2 + len(grads)),
        out_specs=[VMEM] * count,
        scratch_shapes=[
            pltpu.VMEM((rows, width), F32),
            pltpu.VMEM((rest.shape[1], width), BF16),
        ],
        name="second_product",
    )(ids, so_far, rest, *grads)


def total_of(pieces):
    total = pieces[0].astype(F32)
    for piece in pieces[1:]:
        total = total + piece.astype(F32)
    return total


def to_owners(array, axis):
    return lax.all_to_all(array, axis, split_axis=0, concat_axis=0, tiled=True)


def per_device(
    video_query, out_grad, audio_latents, kv_weight, video_length, audio_length, align_list
):
    frames = lax.axis_size("frame")
    audio_count = lax.axis_size("audio")
    clips = lax.axis_size("dp")
    local_width = kv_weight.shape[2]
    latents = audio_latents[0]
    ids = jnp.stack(
        [
            lax.axis_index("audio"),
            lax.axis_index("dp"),
            lax.rem(lax.axis_index("frame"), 2),
            video_length[0],
            audio_length[0],
        ]
    )
    ids = jnp.concatenate([ids, align_list.reshape(-1)]).astype(jnp.int32)
    hops = range(1, audio_count)
    cores = range(frames)
    beside = [(f, f ^ 1) for f in cores]
    around = [
        (f * audio_count + a, f * audio_count + (a + 1 - 2 * (f % 2)) % audio_count)
        for f in cores
        for a in range(audio_count)
    ]
    paired = [
        (c * frames + f, (((c + f % 2) ^ 1) - f % 2) % clips * frames + f)
        for c in range(clips)
        for f in cores
    ]

    packed = pack(video_query[0], out_grad[0], frames)
    arrived = to_owners(packed, "frame")
    projected = jnp.dot(
        latents, kv_weight.reshape(D, 2 * local_width), preferred_element_type=F32
    ).astype(BF16)
    half_rows = projected.shape[0] // 2
    left = shifted(projected, "audio", 1)
    right = shifted(projected, "audio", -1)
    low = shifted(left[:half_rows], "audio", 1)
    high = shifted(right[half_rows:], "audio", -1)
    tables = [projected, left, right, low, high]
    held, near, far = turn(ids, latents, clips, audio_count)
    near = lax.ppermute(near, ("frame", "audio"), around)
    far = shifted(far, "audio", 2)
    paired_held = lax.ppermute(held, ("dp", "frame"), paired)

    results, grads = attend(ids, arrived, tables, audio_count)
    added = [grads[0]]
    for k in hops:
        added.append(shifted(grads[k], "audio", k))
    results = to_owners(results, "frame")
    near_swapped = lax.ppermute(near, "frame", beside)
    far_swapped = lax.ppermute(far, "frame", beside)
    rest = assemble(ids, near, far, near_swapped, far_swapped)
    paired_rest = lax.ppermute(rest, ("dp", "frame"), paired)
    total = total_of(added).astype(BF16)
    mine, theirs = total[:, :local_width], total[:, local_width:]
    came = lax.ppermute(theirs, ("dp", "frame"), paired)
    shares, paired_shares = [mine], [came]
    for k in hops:
        shares.append(shifted(mine, "audio", k))
    for k in hops:
        paired_shares.append(shifted(came, "audio", k))
    so_far = first_product(held, rest, paired_held, came, shares)
    pieces = second_product(
        ids, so_far, paired_rest, paired_shares[1:], clips, 1.0 / clips
    )
    parts = [pieces[0]]
    for k in range(1, clips):
        parts.append(shifted(pieces[k], "dp", k))
    same, other = total_of(parts[::2]), total_of(parts[1::2])
    even = ids[1] % 2 == 0
    weight_grad = jnp.stack(
        [jnp.where(even, other, same), jnp.where(even, same, other)], axis=1
    )
    attended, query_grad = unpack(results)
    return attended[None], query_grad[None], weight_grad


def solution(mesh):
    return jax.shard_map(
        per_device,
        mesh=mesh,
        in_specs=(
            P("dp", ("frame", "audio"), None),
            P("dp", ("frame", "audio"), None),
            P("dp", "audio", None),
            P(None, None, "frame"),
            P("dp"),
            P("dp"),
            P("dp", None, None),
        ),
        out_specs=(
            P("dp", ("frame", "audio"), None),
            P("dp", ("frame", "audio"), None),
            P(("dp", "audio"), None, "frame"),
        ),
        check_vma=False,
    )
```

```python
import jax
import jax.numpy as jnp
from jax import lax
from jax.experimental import pallas as pl
from jax.experimental.pallas import tpu as pltpu
from jax.sharding import PartitionSpec as P


D = 3072
HD = 128
QB = 128
KB = 64
NLIST = 2
SCALING = HD ** (-0.5)
LOG2_E = 1.4426950408889634
BF16 = jnp.bfloat16
F32 = jnp.float32


VMEM = pl.BlockSpec(memory_space=pltpu.VMEM)
SMEM = pl.BlockSpec(memory_space=pltpu.SMEM)
ANY = pl.BlockSpec(memory_space=pl.ANY)


def shifted(array, axis, by):
    count = lax.axis_size(axis)
    return lax.ppermute(array, axis, [(i, (i + by) % count) for i in range(count)])


def pack_kernel(query, grad, out):
    width = out.shape[3]
    for j in range(out.shape[0]):
        out[j, 0] = query[:, j * width : (j + 1) * width]
        out[j, 1] = grad[:, j * width : (j + 1) * width]


def pack(query, grad, frames):
    rows, width = query.shape
    steps = 2
    part = pl.BlockSpec((rows, width // steps), lambda i: (0, i))
    shape = (frames, 2, rows, width // frames)
    return pl.pallas_call(
        pack_kernel,
        grid=(steps,),
        out_shape=jax.ShapeDtypeStruct(shape, query.dtype),
        in_specs=[part, part],
        out_specs=pl.BlockSpec((frames // steps, *shape[1:]), lambda i: (i, 0, 0, 0)),
        name="pack",
    )(query, grad)


def unpack_kernel(pieces, attended, query_grad):
    width = pieces.shape[3]
    for j in range(pieces.shape[0]):
        attended[:, j * width : (j + 1) * width] = pieces[j, 0]
        query_grad[:, j * width : (j + 1) * width] = pieces[j, 1]


def unpack(pieces):
    frames, _, rows, width = pieces.shape
    whole = jax.ShapeDtypeStruct((rows, width * frames), pieces.dtype)
    return pl.pallas_call(
        unpack_kernel,
        out_shape=[whole, whole],
        in_specs=[VMEM],
        out_specs=[VMEM, VMEM],
        name="unpack",
    )(pieces)


def turn_kernel(audio_count, ids, latents, own, near, far, turned):
    rows = turned.shape[0] // audio_count
    count = own.shape[0] // rows
    width = rows * audio_count
    core = ids[2]

    def part(ahead):
        at = lax.rem(ids[0] + ahead, audio_count) * rows
        return turned[pl.ds(pl.multiple_of(at, 16), rows), :]

    for j in range(count):
        turned[...] = latents[:, j * width : (j + 1) * width].T
        own[j * rows : (j + 1) * rows] = part(0)
        near[j * rows : (j + 1) * rows] = part(1 + core * (audio_count - 2))
        half, place = divmod(j, count // 2)

        @pl.when(core == half)
        def _():
            far[place * rows : (place + 1) * rows] = part(2)


def turn(ids, latents, clips, audio_count):
    count, width = latents.shape
    share = width // audio_count

    def kernel(*refs):
        turn_kernel(audio_count, *refs)

    return pl.pallas_call(
        kernel,
        out_shape=[
            jax.ShapeDtypeStruct((share, count), latents.dtype),
            jax.ShapeDtypeStruct((share, count), latents.dtype),
            jax.ShapeDtypeStruct((share // 2, count), latents.dtype),
        ],
        in_specs=[SMEM, VMEM],
        out_specs=[VMEM] * 3,
        scratch_shapes=[pltpu.VMEM((width // clips, count), latents.dtype)],
        name="turn",
    )(ids, latents)


def dot(left, right, left_dim, right_dim):
    return lax.dot_general(
        left, right, (((left_dim,), (right_dim,)), ((), ())), preferred_element_type=F32
    )


def attend_kernel(audio_count, heads, ids, rows_in, *refs):
    refs = list(refs)
    take = lambda n: [refs.pop(0) for _ in range(n)]
    tables, (rows_out,), grads = take(5), take(1), take(audio_count)
    (table,), sums, (table_sem,) = take(1), take(2 * heads), take(1)
    share = tables[0].shape[0]
    here = ids[0]
    step = pl.program_id(0)
    count = rows_in.shape[0]

    @pl.when(step == 0)
    def _():
        copies = []
        places = ((0, 0), (audio_count - 1, 0), (1, 0), (2, 0), (2, share // 2))
        for i, (ahead, extra) in enumerate(places):
            at = lax.rem(here + ahead, audio_count) * share + extra
            at = pl.ds(pl.multiple_of(at, share // 2), tables[i].shape[0])
            copies.append(pltpu.make_async_copy(tables[i], table.at[at, :], table_sem.at[i]))
        for copy in copies:
            copy.start()
        for part in sums:
            part[...] = jnp.zeros_like(part)
        for copy in copies:
            copy.wait()

    key_row = lax.broadcasted_iota(jnp.int32, (NLIST * KB, 1), 0)
    query_lane = lax.broadcasted_iota(jnp.int32, (1, QB), 1)

    def one(k):
        index = (step * count + k) * audio_count + here
        first = pl.multiple_of(ids[5 + NLIST * index] * KB, KB)
        second = pl.multiple_of(ids[6 + NLIST * index] * KB, KB)
        key_index = jnp.where(key_row < KB, first + key_row, second + key_row - KB)
        allowed = key_index < ids[4]
        live = query_lane + index * QB < ids[3]
        parts = []
        for h in range(heads):
            cols = slice(h * HD, (h + 1) * HD)
            vcols = slice((heads + h) * HD, (heads + h + 1) * HD)
            query = rows_in[k, 0, :, cols]
            grad = rows_in[k, 1, :, cols]
            key = jnp.concatenate(
                [table[pl.ds(first, KB), cols], table[pl.ds(second, KB), cols]], axis=0
            )
            value = jnp.concatenate(
                [table[pl.ds(first, KB), vcols], table[pl.ds(second, KB), vcols]], axis=0
            )
            scores = dot(key, query, 1, 1)
            prob_grad = dot(value, grad, 1, 1)
            scores = jnp.where(allowed, scores, -1e30)
            scores = scores - jnp.max(scores, axis=0, keepdims=True)
            weights = jnp.exp2(scores * (SCALING * LOG2_E))
            inverse = 1.0 / jnp.sum(weights, axis=0, keepdims=True)
            probability = weights * jnp.where(live, inverse, 0.0)
            prob_low = probability.astype(BF16)
            row_dot = jnp.sum(probability * prob_grad, axis=0, keepdims=True)
            score_grad = (probability * (prob_grad - row_dot)).astype(BF16)
            output = dot(prob_low, value, 0, 0).astype(BF16)
            query_part = (dot(score_grad, key, 0, 0) * SCALING).astype(BF16)
            key_part = dot(score_grad, query, 1, 0) * SCALING
            value_part = dot(prob_low, grad, 1, 0)
            parts.append((output, query_part, key_part, value_part))
        return first, second, parts

    def finish(k, first, second, parts):
        for h, (output, query_part, key_part, value_part) in enumerate(parts):
            cols = slice(h * HD, (h + 1) * HD)
            rows_out[k, 0, :, cols] = output
            rows_out[k, 1, :, cols] = query_part
            for into, part in ((sums[h], key_part), (sums[heads + h], value_part)):
                into[pl.ds(first, KB), :] += part[:KB]
                into[pl.ds(second, KB), :] += part[KB:]

    made = [(k, *one(k)) for k in range(count)]
    for entry in made:
        finish(*entry)

    @pl.when(step == pl.num_programs(0) - 1)
    def _():
        for k in range(audio_count):
            at = pl.multiple_of(lax.rem(here + k, audio_count) * share, share)
            for c, total in enumerate(sums):
                half, h = divmod(c, heads)
                place = half + (1 - 2 * half) * (1 - lax.rem(ids[1], 2))
                cols = pl.ds(pl.multiple_of((place * heads + h) * HD, HD), HD)
                grads[k][:, cols] = total[pl.ds(at, share), :].astype(grads[k].dtype)


def attend(ids, arrived, tables, audio_count):
    share, width = tables[0].shape
    heads = width // (2 * HD)
    total = share * audio_count
    count = 4
    rows = pl.BlockSpec((count, *arrived.shape[1:]), lambda i: (i, 0, 0, 0))
    part = pl.BlockSpec((share, width), lambda i: (0, 0))

    def kernel(*refs):
        attend_kernel(audio_count, heads, *refs)

    results, *grads = pl.pallas_call(
        kernel,
        grid=(arrived.shape[0] // count,),
        out_shape=[jax.ShapeDtypeStruct(arrived.shape, BF16)]
        + [jax.ShapeDtypeStruct((share, width), F32)]
        + [jax.ShapeDtypeStruct((share, width), BF16)] * (audio_count - 1),
        in_specs=[SMEM, rows] + [ANY] * len(tables),
        out_specs=[rows] + [part] * audio_count,
        scratch_shapes=[pltpu.VMEM((total, width), BF16)]
        + [pltpu.VMEM((total, HD), F32)] * (2 * heads)
        + [pltpu.SemaphoreType.DMA((len(tables),))],
        compiler_params=pltpu.CompilerParams(dimension_semantics=("arbitrary",)),
        name="attend",
    )(ids, arrived, *tables)
    return results, grads


def assemble_kernel(ids, near, far, near_swapped, far_swapped, out):
    half, depth = far.shape
    core = ids[2]
    middle = slice(depth, 2 * depth)
    out[pl.ds(pl.multiple_of(core * half, 16), half), middle] = far[...]
    out[pl.ds(pl.multiple_of((1 - core) * half, 16), half), middle] = far_swapped[...]

    @pl.when(core == 0)
    def _():
        out[:, :depth] = near[...]
        out[:, 2 * depth :] = near_swapped[...]

    @pl.when(core == 1)
    def _():
        out[:, :depth] = near_swapped[...]
        out[:, 2 * depth :] = near[...]


def assemble(ids, near, *parts):
    rows, depth = near.shape
    return pl.pallas_call(
        assemble_kernel,
        out_shape=jax.ShapeDtypeStruct((rows, depth * 3), near.dtype),
        in_specs=[SMEM] + [VMEM] * 4,
        out_specs=VMEM,
        name="assemble",
    )(ids, near, *parts)


def first_product_kernel(held, rest, paired_held, came, *refs):
    grads, (out, table) = refs[:-2], refs[-2:]
    depth = came.shape[0]
    for k, grad in enumerate(grads[1:]):
        table[k * depth : (k + 1) * depth, :] = grad[...]
    total = dot(held[...], grads[0][...], 1, 0) + dot(paired_held[...], came[...], 1, 0)
    out[...] = total + dot(rest[...], table[...], 1, 0)


def first_product(held, rest, paired_held, came, grads):
    shape = (held.shape[0], came.shape[1])
    return pl.pallas_call(
        first_product_kernel,
        out_shape=jax.ShapeDtypeStruct(shape, F32),
        in_specs=[VMEM] * (4 + len(grads)),
        out_specs=VMEM,
        scratch_shapes=[pltpu.VMEM((rest.shape[1], shape[1]), BF16)],
        name="first_product",
    )(held, rest, paired_held, came, *grads)


def second_product_kernel(scale, hops, ids, so_far, rest, *refs):
    grads, outs, (whole, table) = refs[:hops], refs[hops:-2], refs[-2:]
    depth = grads[0].shape[0]
    for k, grad in enumerate(grads):
        table[k * depth : (k + 1) * depth, :] = grad[...]
    whole[...] = (so_far[...] + dot(rest[...], table[...], 1, 0)) * scale
    count, rows = len(outs), outs[0].shape[0]
    for k in range(count):
        at = pl.multiple_of(lax.rem(ids[1] + k, count) * rows, 16)
        outs[k][...] = whole[pl.ds(at, rows), :].astype(outs[k].dtype)


def second_product(ids, so_far, rest, grads, count, scale):
    rows, width = so_far.shape

    def kernel(*refs):
        second_product_kernel(scale, len(grads), *refs)

    shape = (rows // count, width)
    return pl.pallas_call(
        kernel,
        out_shape=[jax.ShapeDtypeStruct(shape, F32)]
        + [jax.ShapeDtypeStruct(shape, BF16)] * (count - 1),
        in_specs=[SMEM] + [VMEM] * (2 + len(grads)),
        out_specs=[VMEM] * count,
        scratch_shapes=[
            pltpu.VMEM((rows, width), F32),
            pltpu.VMEM((rest.shape[1], width), BF16),
        ],
        name="second_product",
    )(ids, so_far, rest, *grads)


def total_of(pieces):
    total = pieces[0].astype(F32)
    for piece in pieces[1:]:
        total = total + piece.astype(F32)
    return total


def to_owners(array, axis):
    return lax.all_to_all(array, axis, split_axis=0, concat_axis=0, tiled=True)


def per_device(
    video_query, out_grad, audio_latents, kv_weight, video_length, audio_length, align_list
):
    frames = lax.axis_size("frame")
    audio_count = lax.axis_size("audio")
    clips = lax.axis_size("dp")
    local_width = kv_weight.shape[2]
    latents = audio_latents[0]
    ids = jnp.stack(
        [
            lax.axis_index("audio"),
            lax.axis_index("dp"),
            lax.rem(lax.axis_index("frame"), 2),
            video_length[0],
            audio_length[0],
        ]
    )
    ids = jnp.concatenate([ids, align_list.reshape(-1)]).astype(jnp.int32)
    hops = range(1, audio_count)
    cores = range(frames)
    beside = [(f, f ^ 1) for f in cores]
    around = [
        (f * audio_count + a, f * audio_count + (a + 1 - 2 * (f % 2)) % audio_count)
        for f in cores
        for a in range(audio_count)
    ]
    paired = [
        (c * frames + f, (((c + f % 2) ^ 1) - f % 2) % clips * frames + f)
        for c in range(clips)
        for f in cores
    ]

    packed = pack(video_query[0], out_grad[0], frames)
    arrived = to_owners(packed, "frame")
    projected = jnp.dot(
        latents, kv_weight.reshape(D, 2 * local_width), preferred_element_type=F32
    ).astype(BF16)
    half_rows = projected.shape[0] // 2
    left = shifted(projected, "audio", 1)
    right = shifted(projected, "audio", -1)
    low = shifted(left[:half_rows], "audio", 1)
    high = shifted(right[half_rows:], "audio", -1)
    tables = [projected, left, right, low, high]
    held, near, far = turn(ids, latents, clips, audio_count)
    near = lax.ppermute(near, ("frame", "audio"), around)
    far = shifted(far, "audio", 2)
    paired_held = lax.ppermute(held, ("dp", "frame"), paired)

    results, grads = attend(ids, arrived, tables, audio_count)
    added = [grads[0]]
    for k in hops:
        added.append(shifted(grads[k], "audio", k))
    results = to_owners(results, "frame")
    near_swapped = lax.ppermute(near, "frame", beside)
    far_swapped = lax.ppermute(far, "frame", beside)
    rest = assemble(ids, near, far, near_swapped, far_swapped)
    paired_rest = lax.ppermute(rest, ("dp", "frame"), paired)
    total = total_of(added).astype(BF16)
    mine, theirs = total[:, :local_width], total[:, local_width:]
    came = lax.ppermute(theirs, ("dp", "frame"), paired)
    shares, paired_shares = [mine], [came]
    for k in hops:
        shares.append(shifted(mine, "audio", k))
    for k in hops:
        paired_shares.append(shifted(came, "audio", k))
    so_far = first_product(held, rest, paired_held, came, shares)
    pieces = second_product(
        ids, so_far, paired_rest, paired_shares[1:], clips, 1.0 / clips
    )
    parts = [pieces[0]]
    for k in range(1, clips):
        parts.append(shifted(pieces[k], "dp", k))
    same, other = total_of(parts[::2]), total_of(parts[1::2])
    even = ids[1] % 2 == 0
    weight_grad = jnp.stack(
        [jnp.where(even, other, same), jnp.where(even, same, other)], axis=1
    )
    attended, query_grad = unpack(results)
    return attended[None], query_grad[None], weight_grad


def solution(mesh):
    return jax.shard_map(
        per_device,
        mesh=mesh,
        in_specs=(
            P("dp", ("frame", "audio"), None),
            P("dp", ("frame", "audio"), None),
            P("dp", "audio", None),
            P(None, None, "frame"),
            P("dp"),
            P("dp"),
            P("dp", None, None),
        ),
        out_specs=(
            P("dp", ("frame", "audio"), None),
            P("dp", ("frame", "audio"), None),
            P(("dp", "audio"), None, "frame"),
        ),
        check_vma=False,
    )
```

```python
import jax
import jax.numpy as jnp
from jax import lax
from jax.experimental import pallas as pl
from jax.experimental.pallas import tpu as pltpu
from jax.sharding import PartitionSpec as P


D = 3072
HD = 128
QB = 128
KB = 64
NLIST = 2
SCALING = HD ** (-0.5)
LOG2_E = 1.4426950408889634
BF16 = jnp.bfloat16
F32 = jnp.float32


VMEM = pl.BlockSpec(memory_space=pltpu.VMEM)
SMEM = pl.BlockSpec(memory_space=pltpu.SMEM)
ANY = pl.BlockSpec(memory_space=pl.ANY)


def shifted(array, axis, by):
    count = lax.axis_size(axis)
    return lax.ppermute(array, axis, [(i, (i + by) % count) for i in range(count)])


def pack_kernel(query, grad, out):
    width = out.shape[3]
    for j in range(out.shape[0]):
        out[j, 0] = query[:, j * width : (j + 1) * width]
        out[j, 1] = grad[:, j * width : (j + 1) * width]


def pack(query, grad, frames):
    rows, width = query.shape
    steps = 2
    part = pl.BlockSpec((rows, width // steps), lambda i: (0, i))
    shape = (frames, 2, rows, width // frames)
    return pl.pallas_call(
        pack_kernel,
        grid=(steps,),
        out_shape=jax.ShapeDtypeStruct(shape, query.dtype),
        in_specs=[part, part],
        out_specs=pl.BlockSpec((frames // steps, *shape[1:]), lambda i: (i, 0, 0, 0)),
        name="pack",
    )(query, grad)


def unpack_kernel(pieces, attended, query_grad):
    width = pieces.shape[3]
    for j in range(pieces.shape[0]):
        attended[:, j * width : (j + 1) * width] = pieces[j, 0]
        query_grad[:, j * width : (j + 1) * width] = pieces[j, 1]


def unpack(pieces):
    frames, _, rows, width = pieces.shape
    whole = jax.ShapeDtypeStruct((rows, width * frames), pieces.dtype)
    return pl.pallas_call(
        unpack_kernel,
        out_shape=[whole, whole],
        in_specs=[VMEM],
        out_specs=[VMEM, VMEM],
        name="unpack",
    )(pieces)


def turn_kernel(audio_count, ids, latents, own, near, far, turned):
    rows = turned.shape[0] // audio_count
    count = own.shape[0] // rows
    width = rows * audio_count
    core = ids[2]

    def part(ahead):
        at = lax.rem(ids[0] + ahead, audio_count) * rows
        return turned[pl.ds(pl.multiple_of(at, 16), rows), :]

    for j in range(count):
        turned[...] = latents[:, j * width : (j + 1) * width].T
        own[j * rows : (j + 1) * rows] = part(0)
        near[j * rows : (j + 1) * rows] = part(1 + core * (audio_count - 2))
        half, place = divmod(j, count // 2)

        @pl.when(core == half)
        def _():
            far[place * rows : (place + 1) * rows] = part(2)


def turn(ids, latents, clips, audio_count):
    count, width = latents.shape
    share = width // audio_count

    def kernel(*refs):
        turn_kernel(audio_count, *refs)

    return pl.pallas_call(
        kernel,
        out_shape=[
            jax.ShapeDtypeStruct((share, count), latents.dtype),
            jax.ShapeDtypeStruct((share, count), latents.dtype),
            jax.ShapeDtypeStruct((share // 2, count), latents.dtype),
        ],
        in_specs=[SMEM, VMEM],
        out_specs=[VMEM] * 3,
        scratch_shapes=[pltpu.VMEM((width // clips, count), latents.dtype)],
        name="turn",
    )(ids, latents)


def dot(left, right, left_dim, right_dim):
    return lax.dot_general(
        left, right, (((left_dim,), (right_dim,)), ((), ())), preferred_element_type=F32
    )


def attend_kernel(audio_count, heads, ids, rows_in, *refs):
    refs = list(refs)
    take = lambda n: [refs.pop(0) for _ in range(n)]
    tables, (rows_out,), grads = take(5), take(1), take(audio_count)
    (table,), sums, (table_sem,) = take(1), take(2 * heads), take(1)
    share = tables[0].shape[0]
    here = ids[0]
    step = pl.program_id(0)
    count = rows_in.shape[0]

    @pl.when(step == 0)
    def _():
        copies = []
        places = ((0, 0), (audio_count - 1, 0), (1, 0), (2, 0), (2, share // 2))
        for i, (ahead, extra) in enumerate(places):
            at = lax.rem(here + ahead, audio_count) * share + extra
            at = pl.ds(pl.multiple_of(at, share // 2), tables[i].shape[0])
            copies.append(pltpu.make_async_copy(tables[i], table.at[at, :], table_sem.at[i]))
        for copy in copies:
            copy.start()
        for part in sums:
            part[...] = jnp.zeros_like(part)
        for copy in copies:
            copy.wait()

    key_row = lax.broadcasted_iota(jnp.int32, (NLIST * KB, 1), 0)
    query_lane = lax.broadcasted_iota(jnp.int32, (1, QB), 1)

    def one(k):
        index = (step * count + k) * audio_count + here
        first = pl.multiple_of(ids[5 + NLIST * index] * KB, KB)
        second = pl.multiple_of(ids[6 + NLIST * index] * KB, KB)
        key_index = jnp.where(key_row < KB, first + key_row, second + key_row - KB)
        allowed = key_index < ids[4]
        live = query_lane + index * QB < ids[3]
        items = []
        for h in range(heads):
            cols = slice(h * HD, (h + 1) * HD)
            vcols = slice((heads + h) * HD, (heads + h + 1) * HD)
            query = rows_in[k, 0, :, cols]
            grad = rows_in[k, 1, :, cols]
            key = jnp.concatenate(
                [table[pl.ds(first, KB), cols], table[pl.ds(second, KB), cols]], axis=0
            )
            value = jnp.concatenate(
                [table[pl.ds(first, KB), vcols], table[pl.ds(second, KB), vcols]], axis=0
            )
            items.append((query, grad, key, value))
        scores = [dot(key, query, 1, 1) for query, _, key, _ in items]
        prob_grads = [dot(value, grad, 1, 1) for _, grad, _, value in items]
        return first, second, allowed, live, items, scores, prob_grads

    def rest_of(first, second, allowed, live, items, scores, prob_grads):
        lows = []
        for score, prob_grad in zip(scores, prob_grads):
            score = jnp.where(allowed, score, -1e30)
            score = score - jnp.max(score, axis=0, keepdims=True)
            weights = jnp.exp2(score * (SCALING * LOG2_E))
            inverse = 1.0 / jnp.sum(weights, axis=0, keepdims=True)
            probability = weights * jnp.where(live, inverse, 0.0)
            row_dot = jnp.sum(probability * prob_grad, axis=0, keepdims=True)
            score_grad = (probability * (prob_grad - row_dot)).astype(BF16)
            lows.append((probability.astype(BF16), score_grad))
        parts = []
        for (query, grad, key, value), (prob_low, score_grad) in zip(items, lows):
            output = dot(prob_low, value, 0, 0).astype(BF16)
            query_part = (dot(score_grad, key, 0, 0) * SCALING).astype(BF16)
            key_part = dot(score_grad, query, 1, 0) * SCALING
            value_part = dot(prob_low, grad, 1, 0)
            parts.append((output, query_part, key_part, value_part))
        return first, second, parts

    def finish(k, first, second, parts):
        for h, (output, query_part, key_part, value_part) in enumerate(parts):
            cols = slice(h * HD, (h + 1) * HD)
            rows_out[k, 0, :, cols] = output
            rows_out[k, 1, :, cols] = query_part
            for into, part in ((sums[h], key_part), (sums[heads + h], value_part)):
                into[pl.ds(first, KB), :] += part[:KB]
                into[pl.ds(second, KB), :] += part[KB:]

    ready = one(0)
    for k in range(count):
        now, ready = ready, one(k + 1) if k + 1 < count else None
        finish(k, *rest_of(*now))

    @pl.when(step == pl.num_programs(0) - 1)
    def _():
        for k in range(audio_count):
            at = pl.multiple_of(lax.rem(here + k, audio_count) * share, share)
            for c, total in enumerate(sums):
                half, h = divmod(c, heads)
                place = half + (1 - 2 * half) * (1 - lax.rem(ids[1], 2))
                cols = pl.ds(pl.multiple_of((place * heads + h) * HD, HD), HD)
                grads[k][:, cols] = total[pl.ds(at, share), :].astype(grads[k].dtype)


def attend(ids, arrived, tables, audio_count):
    share, width = tables[0].shape
    heads = width // (2 * HD)
    total = share * audio_count
    count = 4
    rows = pl.BlockSpec((count, *arrived.shape[1:]), lambda i: (i, 0, 0, 0))
    part = pl.BlockSpec((share, width), lambda i: (0, 0))

    def kernel(*refs):
        attend_kernel(audio_count, heads, *refs)

    results, *grads = pl.pallas_call(
        kernel,
        grid=(arrived.shape[0] // count,),
        out_shape=[jax.ShapeDtypeStruct(arrived.shape, BF16)]
        + [jax.ShapeDtypeStruct((share, width), F32)]
        + [jax.ShapeDtypeStruct((share, width), BF16)] * (audio_count - 1),
        in_specs=[SMEM, rows] + [ANY] * len(tables),
        out_specs=[rows] + [part] * audio_count,
        scratch_shapes=[pltpu.VMEM((total, width), BF16)]
        + [pltpu.VMEM((total, HD), F32)] * (2 * heads)
        + [pltpu.SemaphoreType.DMA((len(tables),))],
        compiler_params=pltpu.CompilerParams(dimension_semantics=("arbitrary",)),
        name="attend",
    )(ids, arrived, *tables)
    return results, grads


def assemble_kernel(ids, near, far, near_swapped, far_swapped, out):
    half, depth = far.shape
    core = ids[2]
    middle = slice(depth, 2 * depth)
    out[pl.ds(pl.multiple_of(core * half, 16), half), middle] = far[...]
    out[pl.ds(pl.multiple_of((1 - core) * half, 16), half), middle] = far_swapped[...]

    @pl.when(core == 0)
    def _():
        out[:, :depth] = near[...]
        out[:, 2 * depth :] = near_swapped[...]

    @pl.when(core == 1)
    def _():
        out[:, :depth] = near_swapped[...]
        out[:, 2 * depth :] = near[...]


def assemble(ids, near, *parts):
    rows, depth = near.shape
    return pl.pallas_call(
        assemble_kernel,
        out_shape=jax.ShapeDtypeStruct((rows, depth * 3), near.dtype),
        in_specs=[SMEM] + [VMEM] * 4,
        out_specs=VMEM,
        name="assemble",
    )(ids, near, *parts)


def first_product_kernel(held, rest, paired_held, came, *refs):
    grads, (out, table) = refs[:-2], refs[-2:]
    depth = came.shape[0]
    for k, grad in enumerate(grads[1:]):
        table[k * depth : (k + 1) * depth, :] = grad[...]
    total = dot(held[...], grads[0][...], 1, 0) + dot(paired_held[...], came[...], 1, 0)
    out[...] = total + dot(rest[...], table[...], 1, 0)


def first_product(held, rest, paired_held, came, grads):
    shape = (held.shape[0], came.shape[1])
    return pl.pallas_call(
        first_product_kernel,
        out_shape=jax.ShapeDtypeStruct(shape, F32),
        in_specs=[VMEM] * (4 + len(grads)),
        out_specs=VMEM,
        scratch_shapes=[pltpu.VMEM((rest.shape[1], shape[1]), BF16)],
        name="first_product",
    )(held, rest, paired_held, came, *grads)


def second_product_kernel(scale, hops, ids, so_far, rest, *refs):
    grads, outs, (whole, table) = refs[:hops], refs[hops:-2], refs[-2:]
    depth = grads[0].shape[0]
    for k, grad in enumerate(grads):
        table[k * depth : (k + 1) * depth, :] = grad[...]
    whole[...] = (so_far[...] + dot(rest[...], table[...], 1, 0)) * scale
    count, rows = len(outs), outs[0].shape[0]
    for k in range(count):
        at = pl.multiple_of(lax.rem(ids[1] + k, count) * rows, 16)
        outs[k][...] = whole[pl.ds(at, rows), :].astype(outs[k].dtype)


def second_product(ids, so_far, rest, grads, count, scale):
    rows, width = so_far.shape

    def kernel(*refs):
        second_product_kernel(scale, len(grads), *refs)

    shape = (rows // count, width)
    return pl.pallas_call(
        kernel,
        out_shape=[jax.ShapeDtypeStruct(shape, F32)]
        + [jax.ShapeDtypeStruct(shape, BF16)] * (count - 1),
        in_specs=[SMEM] + [VMEM] * (2 + len(grads)),
        out_specs=[VMEM] * count,
        scratch_shapes=[
            pltpu.VMEM((rows, width), F32),
            pltpu.VMEM((rest.shape[1], width), BF16),
        ],
        name="second_product",
    )(ids, so_far, rest, *grads)


def total_of(pieces):
    total = pieces[0].astype(F32)
    for piece in pieces[1:]:
        total = total + piece.astype(F32)
    return total


def to_owners(array, axis):
    return lax.all_to_all(array, axis, split_axis=0, concat_axis=0, tiled=True)


def per_device(
    video_query, out_grad, audio_latents, kv_weight, video_length, audio_length, align_list
):
    frames = lax.axis_size("frame")
    audio_count = lax.axis_size("audio")
    clips = lax.axis_size("dp")
    local_width = kv_weight.shape[2]
    latents = audio_latents[0]
    ids = jnp.stack(
        [
            lax.axis_index("audio"),
            lax.axis_index("dp"),
            lax.rem(lax.axis_index("frame"), 2),
            video_length[0],
            audio_length[0],
        ]
    )
    ids = jnp.concatenate([ids, align_list.reshape(-1)]).astype(jnp.int32)
    hops = range(1, audio_count)
    cores = range(frames)
    beside = [(f, f ^ 1) for f in cores]
    around = [
        (f * audio_count + a, f * audio_count + (a + 1 - 2 * (f % 2)) % audio_count)
        for f in cores
        for a in range(audio_count)
    ]
    paired = [
        (c * frames + f, (((c + f % 2) ^ 1) - f % 2) % clips * frames + f)
        for c in range(clips)
        for f in cores
    ]

    packed = pack(video_query[0], out_grad[0], frames)
    arrived = to_owners(packed, "frame")
    projected = jnp.dot(
        latents, kv_weight.reshape(D, 2 * local_width), preferred_element_type=F32
    ).astype(BF16)
    half_rows = projected.shape[0] // 2
    left = shifted(projected, "audio", 1)
    right = shifted(projected, "audio", -1)
    low = shifted(left[:half_rows], "audio", 1)
    high = shifted(right[half_rows:], "audio", -1)
    tables = [projected, left, right, low, high]
    held, near, far = turn(ids, latents, clips, audio_count)
    near = lax.ppermute(near, ("frame", "audio"), around)
    far = shifted(far, "audio", 2)
    paired_held = lax.ppermute(held, ("dp", "frame"), paired)

    results, grads = attend(ids, arrived, tables, audio_count)
    added = [grads[0]]
    for k in hops:
        added.append(shifted(grads[k], "audio", k))
    results = to_owners(results, "frame")
    near_swapped = lax.ppermute(near, "frame", beside)
    far_swapped = lax.ppermute(far, "frame", beside)
    rest = assemble(ids, near, far, near_swapped, far_swapped)
    paired_rest = lax.ppermute(rest, ("dp", "frame"), paired)
    theirs = total_of([part[:, local_width:] for part in added]).astype(BF16)
    mine = total_of([part[:, :local_width] for part in added]).astype(BF16)
    came = lax.ppermute(theirs, ("dp", "frame"), paired)
    shares, paired_shares = [mine], [came]
    for k in hops:
        shares.append(shifted(mine, "audio", k))
    for k in hops:
        paired_shares.append(shifted(came, "audio", k))
    so_far = first_product(held, rest, paired_held, came, shares)
    pieces = second_product(
        ids, so_far, paired_rest, paired_shares[1:], clips, 1.0 / clips
    )
    parts = [pieces[0]]
    for k in range(1, clips):
        parts.append(shifted(pieces[k], "dp", k))
    same, other = total_of(parts[::2]), total_of(parts[1::2])
    even = ids[1] % 2 == 0
    weight_grad = jnp.stack(
        [jnp.where(even, other, same), jnp.where(even, same, other)], axis=1
    )
    attended, query_grad = unpack(results)
    return attended[None], query_grad[None], weight_grad


def solution(mesh):
    return jax.shard_map(
        per_device,
        mesh=mesh,
        in_specs=(
            P("dp", ("frame", "audio"), None),
            P("dp", ("frame", "audio"), None),
            P("dp", "audio", None),
            P(None, None, "frame"),
            P("dp"),
            P("dp"),
            P("dp", None, None),
        ),
        out_specs=(
            P("dp", ("frame", "audio"), None),
            P("dp", ("frame", "audio"), None),
            P(("dp", "audio"), None, "frame"),
        ),
        check_vma=False,
    )
```

```python
import jax
import jax.numpy as jnp
from jax import lax
from jax.experimental import pallas as pl
from jax.experimental.pallas import tpu as pltpu
from jax.sharding import PartitionSpec as P


D = 3072
HD = 128
QB = 128
KB = 64
NLIST = 2
SCALING = HD ** (-0.5)
LOG2_E = 1.4426950408889634
BF16 = jnp.bfloat16
F32 = jnp.float32


VMEM = pl.BlockSpec(memory_space=pltpu.VMEM)
SMEM = pl.BlockSpec(memory_space=pltpu.SMEM)
ANY = pl.BlockSpec(memory_space=pl.ANY)


def shifted(array, axis, by):
    count = lax.axis_size(axis)
    return lax.ppermute(array, axis, [(i, (i + by) % count) for i in range(count)])


def pack_kernel(query, grad, out):
    width = out.shape[3]
    for j in range(out.shape[0]):
        out[j, 0] = query[:, j * width : (j + 1) * width]
        out[j, 1] = grad[:, j * width : (j + 1) * width]


def pack(query, grad, frames):
    rows, width = query.shape
    steps = 2
    part = pl.BlockSpec((rows, width // steps), lambda i: (0, i))
    shape = (frames, 2, rows, width // frames)
    return pl.pallas_call(
        pack_kernel,
        grid=(steps,),
        out_shape=jax.ShapeDtypeStruct(shape, query.dtype),
        in_specs=[part, part],
        out_specs=pl.BlockSpec((frames // steps, *shape[1:]), lambda i: (i, 0, 0, 0)),
        name="pack",
    )(query, grad)


def unpack_kernel(pieces, attended, query_grad):
    width = pieces.shape[3]
    for j in range(pieces.shape[0]):
        attended[:, j * width : (j + 1) * width] = pieces[j, 0]
        query_grad[:, j * width : (j + 1) * width] = pieces[j, 1]


def unpack(pieces):
    frames, _, rows, width = pieces.shape
    whole = jax.ShapeDtypeStruct((rows, width * frames), pieces.dtype)
    return pl.pallas_call(
        unpack_kernel,
        out_shape=[whole, whole],
        in_specs=[VMEM],
        out_specs=[VMEM, VMEM],
        name="unpack",
    )(pieces)


def turn_kernel(audio_count, ids, latents, own, near, far, turned):
    rows = turned.shape[0] // audio_count
    count = own.shape[0] // rows
    width = rows * audio_count
    core = ids[2]

    def part(ahead):
        at = lax.rem(ids[0] + ahead, audio_count) * rows
        return turned[pl.ds(pl.multiple_of(at, 16), rows), :]

    for j in range(count):
        turned[...] = latents[:, j * width : (j + 1) * width].T
        own[j * rows : (j + 1) * rows] = part(0)
        near[j * rows : (j + 1) * rows] = part(1 + core * (audio_count - 2))
        half, place = divmod(j, count // 2)

        @pl.when(core == half)
        def _():
            far[place * rows : (place + 1) * rows] = part(2)


def turn(ids, latents, clips, audio_count):
    count, width = latents.shape
    share = width // audio_count

    def kernel(*refs):
        turn_kernel(audio_count, *refs)

    return pl.pallas_call(
        kernel,
        out_shape=[
            jax.ShapeDtypeStruct((share, count), latents.dtype),
            jax.ShapeDtypeStruct((share, count), latents.dtype),
            jax.ShapeDtypeStruct((share // 2, count), latents.dtype),
        ],
        in_specs=[SMEM, VMEM],
        out_specs=[VMEM] * 3,
        scratch_shapes=[pltpu.VMEM((width // clips, count), latents.dtype)],
        name="turn",
    )(ids, latents)


def dot(left, right, left_dim, right_dim):
    return lax.dot_general(
        left, right, (((left_dim,), (right_dim,)), ((), ())), preferred_element_type=F32
    )


def attend_kernel(audio_count, heads, ids, rows_in, *refs):
    refs = list(refs)
    take = lambda n: [refs.pop(0) for _ in range(n)]
    tables, (rows_out,), grads = take(5), take(1), take(audio_count)
    (table,), sums, (table_sem,) = take(1), take(2 * heads), take(1)
    share = tables[0].shape[0]
    here = ids[0]
    step = pl.program_id(0)
    count = rows_in.shape[0]

    @pl.when(step == 0)
    def _():
        copies = []
        places = ((0, 0), (audio_count - 1, 0), (1, 0), (2, 0), (2, share // 2))
        for i, (ahead, extra) in enumerate(places):
            at = lax.rem(here + ahead, audio_count) * share + extra
            at = pl.ds(pl.multiple_of(at, share // 2), tables[i].shape[0])
            copies.append(pltpu.make_async_copy(tables[i], table.at[at, :], table_sem.at[i]))
        for copy in copies:
            copy.start()
        for part in sums:
            part[...] = jnp.zeros_like(part)
        for copy in copies:
            copy.wait()

    key_row = lax.broadcasted_iota(jnp.int32, (NLIST * KB, 1), 0)
    query_lane = lax.broadcasted_iota(jnp.int32, (1, QB), 1)

    def one(k):
        index = (step * count + k) * audio_count + here
        first = pl.multiple_of(ids[5 + NLIST * index] * KB, KB)
        second = pl.multiple_of(ids[6 + NLIST * index] * KB, KB)
        key_index = jnp.where(key_row < KB, first + key_row, second + key_row - KB)
        allowed = key_index < ids[4]
        live = query_lane + index * QB < ids[3]
        items = []
        for h in range(heads):
            cols = slice(h * HD, (h + 1) * HD)
            vcols = slice((heads + h) * HD, (heads + h + 1) * HD)
            query = rows_in[k, 0, :, cols]
            grad = rows_in[k, 1, :, cols]
            key = jnp.concatenate(
                [table[pl.ds(first, KB), cols], table[pl.ds(second, KB), cols]], axis=0
            )
            value = jnp.concatenate(
                [table[pl.ds(first, KB), vcols], table[pl.ds(second, KB), vcols]], axis=0
            )
            items.append((query, grad, key, value))
        scores = [dot(key, query, 1, 1) for query, _, key, _ in items]
        prob_grads = [dot(value, grad, 1, 1) for _, grad, _, value in items]
        return first, second, allowed, live, items, scores, prob_grads

    def rest_of(first, second, allowed, live, items, scores, prob_grads):
        lows = []
        for score, prob_grad in zip(scores, prob_grads):
            score = jnp.where(allowed, score, -1e30)
            score = score - jnp.max(score, axis=0, keepdims=True)
            weights = jnp.exp2(score * (SCALING * LOG2_E))
            inverse = 1.0 / jnp.sum(weights, axis=0, keepdims=True)
            probability = weights * jnp.where(live, inverse, 0.0)
            row_dot = jnp.sum(probability * prob_grad, axis=0, keepdims=True)
            score_grad = (probability * (prob_grad - row_dot)).astype(BF16)
            lows.append((probability.astype(BF16), score_grad))
        parts = []
        for (query, grad, key, value), (prob_low, score_grad) in zip(items, lows):
            output = dot(prob_low, value, 0, 0).astype(BF16)
            query_part = (dot(score_grad, key, 0, 0) * SCALING).astype(BF16)
            key_part = dot(score_grad, query, 1, 0) * SCALING
            value_part = dot(prob_low, grad, 1, 0)
            parts.append((output, query_part, key_part, value_part))
        return first, second, parts

    def finish(k, first, second, parts):
        for h, (output, query_part, key_part, value_part) in enumerate(parts):
            cols = slice(h * HD, (h + 1) * HD)
            rows_out[k, 0, :, cols] = output
            rows_out[k, 1, :, cols] = query_part
            for into, part in ((sums[h], key_part), (sums[heads + h], value_part)):
                into[pl.ds(first, KB), :] += part[:KB]
                into[pl.ds(second, KB), :] += part[KB:]

    ready = one(0)
    for k in range(count):
        now, ready = ready, one(k + 1) if k + 1 < count else None
        finish(k, *rest_of(*now))

    @pl.when(step == pl.num_programs(0) - 1)
    def _():
        for k in range(audio_count):
            at = pl.multiple_of(lax.rem(here + k, audio_count) * share, share)
            for c, total in enumerate(sums):
                half, h = divmod(c, heads)
                place = half + (1 - 2 * half) * (1 - lax.rem(ids[1], 2))
                cols = pl.ds(pl.multiple_of((place * heads + h) * HD, HD), HD)
                grads[k][:, cols] = total[pl.ds(at, share), :].astype(grads[k].dtype)


def attend(ids, arrived, tables, audio_count):
    share, width = tables[0].shape
    heads = width // (2 * HD)
    total = share * audio_count
    count = 4
    rows = pl.BlockSpec((count, *arrived.shape[1:]), lambda i: (i, 0, 0, 0))
    part = pl.BlockSpec((share, width), lambda i: (0, 0))

    def kernel(*refs):
        attend_kernel(audio_count, heads, *refs)

    results, *grads = pl.pallas_call(
        kernel,
        grid=(arrived.shape[0] // count,),
        out_shape=[jax.ShapeDtypeStruct(arrived.shape, BF16)]
        + [jax.ShapeDtypeStruct((share, width), F32)]
        + [jax.ShapeDtypeStruct((share, width), BF16)] * (audio_count - 1),
        in_specs=[SMEM, rows] + [ANY] * len(tables),
        out_specs=[rows] + [part] * audio_count,
        scratch_shapes=[pltpu.VMEM((total, width), BF16)]
        + [pltpu.VMEM((total, HD), F32)] * (2 * heads)
        + [pltpu.SemaphoreType.DMA((len(tables),))],
        compiler_params=pltpu.CompilerParams(dimension_semantics=("arbitrary",)),
        name="attend",
    )(ids, arrived, *tables)
    return results, grads


def assemble_kernel(ids, near, far, near_swapped, far_swapped, out):
    half, depth = far.shape
    core = ids[2]
    middle = slice(depth, 2 * depth)
    out[pl.ds(pl.multiple_of(core * half, 16), half), middle] = far[...]
    out[pl.ds(pl.multiple_of((1 - core) * half, 16), half), middle] = far_swapped[...]

    @pl.when(core == 0)
    def _():
        out[:, :depth] = near[...]
        out[:, 2 * depth :] = near_swapped[...]

    @pl.when(core == 1)
    def _():
        out[:, :depth] = near_swapped[...]
        out[:, 2 * depth :] = near[...]


def assemble(ids, near, *parts):
    rows, depth = near.shape
    return pl.pallas_call(
        assemble_kernel,
        out_shape=jax.ShapeDtypeStruct((rows, depth * 3), near.dtype),
        in_specs=[SMEM] + [VMEM] * 4,
        out_specs=VMEM,
        name="assemble",
    )(ids, near, *parts)


def first_product_kernel(held, rest, paired_held, came, *refs):
    grads, (out, table) = refs[:-2], refs[-2:]
    depth = came.shape[0]
    for k, grad in enumerate(grads[1:]):
        table[k * depth : (k + 1) * depth, :] = grad[...]
    total = dot(held[...], grads[0][...], 1, 0) + dot(paired_held[...], came[...], 1, 0)
    out[...] = total + dot(rest[...], table[...], 1, 0)


def first_product(held, rest, paired_held, came, grads):
    shape = (held.shape[0], came.shape[1])
    return pl.pallas_call(
        first_product_kernel,
        out_shape=jax.ShapeDtypeStruct(shape, F32),
        in_specs=[VMEM] * (4 + len(grads)),
        out_specs=VMEM,
        scratch_shapes=[pltpu.VMEM((rest.shape[1], shape[1]), BF16)],
        name="first_product",
    )(held, rest, paired_held, came, *grads)


def second_product_kernel(scale, hops, ids, so_far, rest, *refs):
    grads, outs, (whole, table) = refs[:hops], refs[hops:-2], refs[-2:]
    depth = grads[0].shape[0]
    for k, grad in enumerate(grads):
        table[k * depth : (k + 1) * depth, :] = grad[...]
    whole[...] = (so_far[...] + dot(rest[...], table[...], 1, 0)) * scale
    count, rows = len(outs), outs[0].shape[0]
    for k in range(count):
        at = pl.multiple_of(lax.rem(ids[1] + k, count) * rows, 16)
        outs[k][...] = whole[pl.ds(at, rows), :].astype(outs[k].dtype)


def second_product(ids, so_far, rest, grads, count, scale):
    rows, width = so_far.shape

    def kernel(*refs):
        second_product_kernel(scale, len(grads), *refs)

    shape = (rows // count, width)
    return pl.pallas_call(
        kernel,
        out_shape=[jax.ShapeDtypeStruct(shape, F32)]
        + [jax.ShapeDtypeStruct(shape, BF16)] * (count - 1),
        in_specs=[SMEM] + [VMEM] * (2 + len(grads)),
        out_specs=[VMEM] * count,
        scratch_shapes=[
            pltpu.VMEM((rows, width), F32),
            pltpu.VMEM((rest.shape[1], width), BF16),
        ],
        name="second_product",
    )(ids, so_far, rest, *grads)


def total_of(pieces):
    total = pieces[0].astype(F32)
    for piece in pieces[1:]:
        total = total + piece.astype(F32)
    return total


def to_owners(array, axis):
    return lax.all_to_all(array, axis, split_axis=0, concat_axis=0, tiled=True)


def per_device(
    video_query, out_grad, audio_latents, kv_weight, video_length, audio_length, align_list
):
    frames = lax.axis_size("frame")
    audio_count = lax.axis_size("audio")
    clips = lax.axis_size("dp")
    local_width = kv_weight.shape[2]
    latents = audio_latents[0]
    ids = jnp.stack(
        [
            lax.axis_index("audio"),
            lax.axis_index("dp"),
            lax.rem(lax.axis_index("frame"), 2),
            video_length[0],
            audio_length[0],
        ]
    )
    ids = jnp.concatenate([ids, align_list.reshape(-1)]).astype(jnp.int32)
    hops = range(1, audio_count)
    cores = range(frames)
    beside = [(f, f ^ 1) for f in cores]
    around = [
        (f * audio_count + a, f * audio_count + (a + 1 - 2 * (f % 2)) % audio_count)
        for f in cores
        for a in range(audio_count)
    ]
    paired = [
        (c * frames + f, (((c + f % 2) ^ 1) - f % 2) % clips * frames + f)
        for c in range(clips)
        for f in cores
    ]

    packed = pack(video_query[0], out_grad[0], frames)
    arrived = to_owners(packed, "frame")
    projected = jnp.dot(
        latents, kv_weight.reshape(D, 2 * local_width), preferred_element_type=F32
    ).astype(BF16)
    half_rows = projected.shape[0] // 2
    left = shifted(projected, "audio", 1)
    right = shifted(projected, "audio", -1)
    low = shifted(left[:half_rows], "audio", 1)
    high = shifted(right[half_rows:], "audio", -1)
    tables = [projected, left, right, low, high]
    held, near, far = turn(ids, latents, clips, audio_count)
    near = lax.ppermute(near, ("frame", "audio"), around)
    far = shifted(far, "audio", 2)
    paired_held = lax.ppermute(held, ("dp", "frame"), paired)

    arrived = pltpu.with_memory_space_constraint(arrived, pltpu.VMEM)
    results, grads = attend(ids, arrived, tables, audio_count)
    added = [grads[0]]
    for k in hops:
        added.append(shifted(grads[k], "audio", k))
    results = to_owners(results, "frame")
    near_swapped = lax.ppermute(near, "frame", beside)
    far_swapped = lax.ppermute(far, "frame", beside)
    rest = assemble(ids, near, far, near_swapped, far_swapped)
    paired_rest = lax.ppermute(rest, ("dp", "frame"), paired)
    theirs = total_of([part[:, local_width:] for part in added]).astype(BF16)
    mine = total_of([part[:, :local_width] for part in added]).astype(BF16)
    came = lax.ppermute(theirs, ("dp", "frame"), paired)
    shares, paired_shares = [mine], [came]
    for k in hops:
        shares.append(shifted(mine, "audio", k))
    for k in hops:
        paired_shares.append(shifted(came, "audio", k))
    near_by = lambda arrays: [
        pltpu.with_memory_space_constraint(array, pltpu.VMEM) for array in arrays
    ]
    shares[1:], paired_shares[1:] = near_by(shares[1:]), near_by(paired_shares[1:])
    so_far = first_product(held, rest, paired_held, came, shares)
    pieces = second_product(
        ids, so_far, paired_rest, paired_shares[1:], clips, 1.0 / clips
    )
    parts = [pieces[0]]
    for k in range(1, clips):
        parts.append(shifted(pieces[k], "dp", k))
    same, other = total_of(parts[::2]), total_of(parts[1::2])
    even = ids[1] % 2 == 0
    weight_grad = jnp.stack(
        [jnp.where(even, other, same), jnp.where(even, same, other)], axis=1
    )
    attended, query_grad = unpack(results)
    return attended[None], query_grad[None], weight_grad


def solution(mesh):
    return jax.shard_map(
        per_device,
        mesh=mesh,
        in_specs=(
            P("dp", ("frame", "audio"), None),
            P("dp", ("frame", "audio"), None),
            P("dp", "audio", None),
            P(None, None, "frame"),
            P("dp"),
            P("dp"),
            P("dp", None, None),
        ),
        out_specs=(
            P("dp", ("frame", "audio"), None),
            P("dp", ("frame", "audio"), None),
            P(("dp", "audio"), None, "frame"),
        ),
        check_vma=False,
    )
```
